256 devices in a mesh: ctx: 32 (over z, y_lo, core), hg: 8 (over x, y_hi).
Axes of the slice: x: 4, y: 4 (y_hi: 2, y_lo: 2; y = y_hi * 2 + y_lo), z: 8, core: 2. Of those that a mesh axis runs over, the one named last changes fastest.
Arguments:
- query_latent_plain: bfloat16 [4096, 128, 512], P('ctx', 'hg'), may hold values from -40 to 40
- query_rope: bfloat16 [4096, 128, 64], P('ctx', 'hg'), may hold values from -40 to 40
- latent_nope: bfloat16 [4096, 512], P('ctx'), may hold values from -6 to 6
- latent_rope: bfloat16 [4096, 64], P('ctx'), may hold values from -6 to 6
- latent_output_gradient: bfloat16 [4096, 128, 512], P('ctx', 'hg'), may hold values from -5 to 5
- block_mask: int32 [64, 64], replicated, may hold values from 0 to 1, as said below
Outputs:
- d_query_nope: bfloat16 [4096, 128, 512], P('ctx', 'hg')
- d_query_rope: bfloat16 [4096, 128, 64], P('ctx', 'hg')
- d_latent_nope: float32 [4096, 512], P(('ctx', 'hg'))
- d_latent_rope: float32 [4096, 64], P(('ctx', 'hg'))
The draws below stay inside these ranges and needn't reach their ends.
Inputs may be any that keep to these rules, and one draw needn't show every extreme that they name: Every mask block may attend to itself: block_mask[b, b] = 1.
All inputs are finite; a program needn't handle non-finite values.
Results may differ from the reference program's by a relative error of at most 0.012.
Values may be sent and summed in bfloat16 or wider, within the bound.
No kernel may reach another device: no remote copies, remote signals or barrier semaphores. Data moves between devices by JAX's collectives and lax.ppermute only.
A program may use at most 64 MiB of HBM per device.

```python
import jax
import jax.numpy as jnp
from jax import lax

LATENT_WIDTH = 512
ROTARY_WIDTH = 64
QUERY_PER_SLOT = 128
WINDOW = 4
HEAD_COUNT = 128
TOKEN_COUNT = 4096
BLK = 64
BLOCKS = 64
N_CTX = 32


def latent_pair(key):
    drawn_part = jax.random.truncated_normal(jax.random.fold_in(key, 11), -4.0, 4.0, (TOKEN_COUNT, LATENT_WIDTH), jnp.float32)
    rope = jax.random.truncated_normal(jax.random.fold_in(key, 12), -4.0, 4.0, (TOKEN_COUNT, ROTARY_WIDTH), jnp.float32)
    return (drawn_part, rope)


def draw_latent_nope(key, part):
    return latent_pair(key)[0].astype(jnp.bfloat16)


def draw_latent_rope(key, part):
    return latent_pair(key)[1].astype(jnp.bfloat16)


def draw_query_latent_plain(key, part):
    base_offset = jax.random.truncated_normal(jax.random.fold_in(key, 21), -4.0, 4.0, (TOKEN_COUNT, HEAD_COUNT, LATENT_WIDTH), jnp.float32)
    return base_offset.astype(jnp.bfloat16)


def draw_query_rope(key, part):
    base_offset = jax.random.truncated_normal(jax.random.fold_in(key, 22), -4.0, 4.0, (TOKEN_COUNT, HEAD_COUNT, ROTARY_WIDTH), jnp.float32)
    return base_offset.astype(jnp.bfloat16)


def draw_block_mask(key, part):
    order = jax.random.permutation(jax.random.fold_in(key, 41), N_CTX).astype(jnp.int32)
    blocks = jnp.arange(BLOCKS, dtype=jnp.int32)
    owner = order[blocks // 2]
    place = jnp.where(blocks % 2 == 0, owner, 2 * N_CTX - 1 - owner)
    keep = jax.random.randint(jax.random.fold_in(key, 42), (BLOCKS, BLOCKS), 0, 4) > 0
    earlier = place[None, :] <= place[:, None]
    same = place[None, :] == place[:, None]
    return (earlier & (keep | same)).astype(jnp.int32)


def shard_levels(key, dims, shards, smallest, high):
    def one(axis_at, shards_of):
        steps = jax.random.uniform(jax.random.fold_in(jax.random.fold_in(key, 6), axis_at), (shards_of,), jnp.float32, smallest / len(shards), high / len(shards))
        return jnp.repeat(jnp.exp(steps), dims[axis_at] // shards_of).reshape((-1,) + (1,) * (len(dims) - axis_at - 1))

    loudness = one(*shards[0])
    for cut in shards[1:]:
        loudness = loudness * one(*cut)
    return loudness


def normal_values(rng, shape, spread, limit, cuts=(), held_as=jnp.bfloat16):
    values = spread * jax.random.normal(rng, shape, jnp.float32)
    if cuts:
        values = values * shard_levels(rng, shape, cuts, -0.22, 0.18)
    return jnp.clip(values, -limit, limit).astype(held_as)


def setup_inputs(seed: int = 0) -> dict:
    splits = jax.random.split(jax.random.key(seed), 7)
    query_latent_plain = draw_query_latent_plain(jax.random.fold_in(splits[6], 71), 0)
    query_rope = draw_query_rope(jax.random.fold_in(splits[6], 71), 0)
    latent_nope = draw_latent_nope(jax.random.fold_in(splits[6], 71), 0)
    latent_rope = draw_latent_rope(jax.random.fold_in(splits[6], 71), 0)
    latent_output_gradient = normal_values(splits[4], (TOKEN_COUNT, HEAD_COUNT, LATENT_WIDTH), 1.0, 5.0, ((0, 32), (1, 8)))
    block_mask = draw_block_mask(jax.random.fold_in(splits[6], 71), 0)
    return {"query_latent_plain": query_latent_plain, "query_rope": query_rope, "latent_nope": latent_nope, "latent_rope": latent_rope, "latent_output_gradient": latent_output_gradient, "block_mask": block_mask}


SCORE_SCALE = 192.0 ** -0.5


def reference(query_latent_plain, query_rope, latent_nope, latent_rope, latent_output_gradient, block_mask):
    row_count = QUERY_PER_SLOT * HEAD_COUNT

    def one_cycle(carry, cycle):
        plain_gradient, rotary_gradient = carry
        start_index = cycle * QUERY_PER_SLOT
        query_plain = lax.dynamic_slice_in_dim(query_latent_plain, start_index, QUERY_PER_SLOT, 0).reshape(row_count, LATENT_WIDTH)
        q_rope = lax.dynamic_slice_in_dim(query_rope, start_index, QUERY_PER_SLOT, 0).reshape(row_count, ROTARY_WIDTH)
        output_gradient_rows = lax.dynamic_slice_in_dim(latent_output_gradient, start_index, QUERY_PER_SLOT, 0).reshape(row_count, LATENT_WIDTH)
        sources = (cycle - jnp.arange(WINDOW, dtype=jnp.int32)) % N_CTX
        key_tokens = (sources[:, None] * QUERY_PER_SLOT + jnp.arange(QUERY_PER_SLOT, dtype=jnp.int32)[None, :]).reshape(-1)
        k_nope = latent_nope[key_tokens]
        k_rope = latent_rope[key_tokens]
        row_block = 2 * cycle + (jnp.arange(row_count, dtype=jnp.int32) // HEAD_COUNT) // BLK
        key_block = (2 * sources[:, None] + jnp.arange(QUERY_PER_SLOT, dtype=jnp.int32)[None, :] // BLK).reshape(-1)
        allowed = block_mask[row_block][:, key_block] == 1
        scores = (jnp.dot(query_plain, k_nope.T, preferred_element_type=jnp.float32)
                  + jnp.dot(q_rope, k_rope.T, preferred_element_type=jnp.float32)) * SCORE_SCALE
        masked = jnp.where(allowed, scores, -jnp.inf)
        top = jnp.max(masked, axis=1)
        lse = top + jnp.log(jnp.sum(jnp.exp(masked - top[:, None]), axis=1))
        prob = jnp.exp(masked - lse[:, None])
        dprob = jnp.dot(output_gradient_rows, k_nope.T, preferred_element_type=jnp.float32)
        delta = jnp.sum(prob * dprob, axis=1)
        dscore = (prob * (dprob - delta[:, None])).astype(jnp.bfloat16)
        prob_low = prob.astype(jnp.bfloat16)
        query_plain_gradient = (SCORE_SCALE * jnp.dot(dscore, k_nope, preferred_element_type=jnp.float32)).astype(jnp.bfloat16)
        query_rotary_gradient = (SCORE_SCALE * jnp.dot(dscore, k_rope, preferred_element_type=jnp.float32)).astype(jnp.bfloat16)
        dk_nope = SCORE_SCALE * jnp.dot(dscore.T, query_plain, preferred_element_type=jnp.float32) + jnp.dot(prob_low.T, output_gradient_rows, preferred_element_type=jnp.float32)
        dk_rope = SCORE_SCALE * jnp.dot(dscore.T, q_rope, preferred_element_type=jnp.float32)
        plain_gradient = plain_gradient.at[key_tokens].add(dk_nope)
        rotary_gradient = rotary_gradient.at[key_tokens].add(dk_rope)
        return (plain_gradient, rotary_gradient), (query_plain_gradient.reshape(QUERY_PER_SLOT, HEAD_COUNT, LATENT_WIDTH), query_rotary_gradient.reshape(QUERY_PER_SLOT, HEAD_COUNT, ROTARY_WIDTH))

    initial_state = (jnp.zeros((TOKEN_COUNT, LATENT_WIDTH), jnp.float32), jnp.zeros((TOKEN_COUNT, ROTARY_WIDTH), jnp.float32))
    (plain_gradient, rotary_gradient), (query_plain_gradient, query_rotary_gradient) = lax.scan(one_cycle, initial_state, jnp.arange(N_CTX, dtype=jnp.int32))
    return (query_plain_gradient.reshape(TOKEN_COUNT, HEAD_COUNT, LATENT_WIDTH), query_rotary_gradient.reshape(TOKEN_COUNT, HEAD_COUNT, ROTARY_WIDTH), plain_gradient, rotary_gradient)
```

```python
import functools

import jax
import jax.numpy as jnp
from jax import lax
from jax.experimental import pallas as pl
from jax.experimental.pallas import tpu as pltpu
from jax.sharding import PartitionSpec as P

SCALE = 192.0 ** (-0.5)
LOG2E = 1.4426950408889634
F32, BF16 = jnp.float32, jnp.bfloat16
TOK = 128
ROPE = 64
WIDE = 640
VM = pltpu.VMEM


def moved(block, sizes, source):
    n_c, n_h = sizes
    route = []
    for c in range(n_c):
        for h in range(n_h):
            sc, sh = source(c, h)
            route.append(((sc % n_c) * n_h + sh % n_h, c * n_h + h))
    return lax.ppermute(block, ("ctx", "hg"), route)


def far_source(c):
    return c - 1 if c % 2 else c - 3


def far_home(c):
    return c + 3 if c % 2 else c + 1


def slot_cycles(me, n):
    odd = lax.rem(me, 2)
    far = me - 3 + 2 * odd
    swp = me - 1 - 2 * odd
    return [lax.rem(x + n, n) for x in (me, me - 2, far, swp)]


def pack_kernel(nope, rope_t, out):
    out[0:TOK, :] = nope[...]
    for j in range(4):
        out[TOK : TOK + 16, 128 * j : 128 * j + 128] = rope_t[16 * j : 16 * j + 16, :]


def main_kernel(
    n_ctx, steps, mask, q, qr, do, own, two, far, swp,
    dst, kcat, kr, own_same, own_other, two_out, far_same, far_other, swp_out, acc, accr,
):
    i = pl.program_id(0)
    me_c = lax.axis_index("ctx")
    me_h = lax.axis_index("hg")

    @pl.when(i == 0)
    def _():
        for s, ref in enumerate((own, two, far, swp)):
            kcat[TOK * s : TOK * s + TOK, :] = ref[0:TOK, :]
            rope_t = jnp.concatenate(
                [ref[TOK : TOK + 16, 128 * j : 128 * j + 128].astype(F32) for j in range(4)], axis=0
            )
            kr[TOK * s : TOK * s + TOK, :] = rope_t.T.astype(BF16)
        acc[...] = jnp.zeros_like(acc)
        accr[...] = jnp.zeros_like(accr)

    nt = (((1,), (1,)), ((), ()))
    s_t = lax.dot_general(kcat[...], q[...], nt, preferred_element_type=F32)
    s_t += lax.dot_general(kr[...], qr[...], nt, preferred_element_type=F32)
    d_t = lax.dot_general(kcat[...], do[...], nt, preferred_element_type=F32)
    row_block = 2 * me_c + i // (steps // 2)
    parts = []
    for s, src in enumerate(slot_cycles(me_c, n_ctx)):
        for b in range(2):
            bias = jnp.where(mask[row_block, 2 * src + b] == 1, 0.0, -1e30).astype(F32)
            at = TOK * s + 64 * b
            parts.append(s_t[at : at + 64, :] * (SCALE * LOG2E) + bias)
    s_t = jnp.concatenate(parts, axis=0)
    e = jnp.exp2(s_t - jnp.max(s_t, axis=0, keepdims=True))
    inv = 1.0 / jnp.sum(e, axis=0, keepdims=True)
    delta = jnp.sum(e * d_t, axis=0, keepdims=True) * inv
    p = e * inv
    ds = (p * ((d_t - delta) * SCALE)).astype(BF16)
    dst[...] = ds
    acc[...] += jnp.dot(ds, q[...], preferred_element_type=F32) + jnp.dot(
        p.astype(BF16), do[...], preferred_element_type=F32
    )
    accr[...] += jnp.dot(ds, qr[...], preferred_element_type=F32)

    @pl.when(i == steps - 1)
    def _():
        me_x, me_y = me_h // 2, lax.rem(me_h, 2)

        def put(out, at, slot, y):
            for k in range(4):
                x = lax.rem(me_x + k, 4)
                row = pl.multiple_of(TOK * slot + (2 * x + y) * 16, 16)
                to = at + 16 * k
                out[to : to + 16, 0:512] = acc[pl.ds(row, 16), :].astype(out.dtype)
                out[to : to + 16, 512 : 512 + ROPE] = accr[pl.ds(row, 16), :].astype(out.dtype)
                out[to : to + 16, 512 + ROPE : WIDE] = jnp.zeros((16, WIDE - 512 - ROPE), out.dtype)

        put(swp_out, 0, 3, me_y)
        put(swp_out, 64, 3, 1 - me_y)
        put(far_same, 0, 2, me_y)
        put(far_other, 0, 2, 1 - me_y)
        put(two_out, 0, 1, me_y)
        put(two_out, 64, 1, 1 - me_y)
        put(own_same, 0, 0, me_y)
        put(own_other, 0, 0, 1 - me_y)


def dq_kernel(dst, kcat, kr, dq, dqr):
    tn = (((0,), (0,)), ((), ()))
    dq[...] = lax.dot_general(dst[...], kcat[...], tn, preferred_element_type=F32).astype(BF16)
    dqr[...] = lax.dot_general(dst[...], kr[...], tn, preferred_element_type=F32).astype(BF16)


def whole(shape):
    return pl.BlockSpec(shape, lambda i: (0,) * len(shape), pipeline_mode=pl.Buffered(1))


def attend(block_mask, q, qr, do, slots, n_ctx):
    rows, width = q.shape
    rb = 512
    steps = rows // rb
    keys = 4 * TOK
    outs = [
        ((keys, rows), BF16, pl.BlockSpec((keys, rb), lambda i: (0, i))),
        ((keys, width), BF16, whole((keys, width))),
        ((keys, ROPE), BF16, whole((keys, ROPE))),
    ] + [
        (s, t, whole(s))
        for s, t in (
            ((64, WIDE), F32), ((64, WIDE), BF16), ((TOK, WIDE), F32),
            ((64, WIDE), BF16), ((64, WIDE), BF16), ((TOK, WIDE), BF16),
        )
    ]
    return pl.pallas_call(
        functools.partial(main_kernel, n_ctx, steps),
        name="attend",
        grid=(steps,),
        in_specs=[
            pl.BlockSpec(memory_space=pltpu.SMEM),
            pl.BlockSpec((rb, width), lambda i: (i, 0)),
            pl.BlockSpec((rb, ROPE), lambda i: (i, 0)),
            pl.BlockSpec((rb, width), lambda i: (i, 0)),
        ]
        + [whole(s.shape) for s in slots],
        out_specs=[o[2] for o in outs],
        out_shape=[jax.ShapeDtypeStruct(o[0], o[1]) for o in outs],
        scratch_shapes=[VM((keys, width), F32), VM((keys, ROPE), F32)],
        compiler_params=pltpu.CompilerParams(vmem_limit_bytes=48 << 20),
        cost_estimate=pl.CostEstimate(flops=5_400_000_000, bytes_accessed=9_000_000, transcendentals=1 << 20),
    )(block_mask, q, qr, do, *slots)


def query_gradient(dst, kcat, kr):
    keys, rows = dst.shape
    width = kcat.shape[1]
    rb = 512
    return pl.pallas_call(
        dq_kernel,
        name="query_gradient",
        grid=(rows // rb,),
        in_specs=[pl.BlockSpec((keys, rb), lambda i: (0, i)), whole(kcat.shape), whole(kr.shape)],
        out_specs=[pl.BlockSpec((rb, width), lambda i: (i, 0)), pl.BlockSpec((rb, ROPE), lambda i: (i, 0))],
        out_shape=[jax.ShapeDtypeStruct((rows, width), BF16), jax.ShapeDtypeStruct((rows, ROPE), BF16)],
        compiler_params=pltpu.CompilerParams(vmem_limit_bytes=32 << 20),
        cost_estimate=pl.CostEstimate(flops=2_400_000_000, bytes_accessed=5_000_000, transcendentals=0),
    )(dst, kcat, kr)


def on_device(query_latent_plain, query_rope, latent_nope, latent_rope, latent_output_gradient, block_mask):
    tokens, heads, width = query_latent_plain.shape
    rows = tokens * heads
    sizes = (lax.axis_size("ctx"), lax.axis_size("hg"))
    send = functools.partial(moved, sizes=sizes)
    own = pl.pallas_call(
        pack_kernel, name="pack", out_shape=jax.ShapeDtypeStruct((TOK + 16, width), BF16)
    )(latent_nope, latent_rope.T)
    two = send(own, source=lambda c, h: (c - 2, h))
    far = send(own, source=lambda c, h: (far_source(c), h))
    swp = send(two, source=lambda c, h: (c ^ 1, h))
    dst, kcat, kr, own_same, own_other, two_dk, far_same, far_other, swp_dk = attend(
        block_mask,
        query_latent_plain.reshape(rows, width),
        query_rope.reshape(rows, ROPE),
        latent_output_gradient.reshape(rows, width),
        (own, two, far, swp),
        sizes[0],
    )
    got_swp = send(swp_dk, source=lambda c, h: (c ^ 1, h))
    got_far = send(far_same, source=lambda c, h: (far_home(c), h))
    got_far_y = send(far_other, source=lambda c, h: (far_home(c), h ^ 1))
    got_own_y = send(own_other, source=lambda c, h: (c, h ^ 1))
    dq, dqr = query_gradient(dst, kcat, kr)
    two_same = (two_dk[:64] + got_swp[:64].astype(F32)).astype(BF16)
    two_other = (two_dk[64:] + got_swp[64:].astype(F32)).astype(BF16)
    got_two = send(two_same, source=lambda c, h: (c + 2, h))
    got_two_y = send(two_other, source=lambda c, h: (c + 2, h ^ 1))
    total = own_same
    for got in (got_far, got_far_y, got_own_y, got_two, got_two_y):
        total = total + got.astype(F32)
    low = total[16:].astype(BF16)
    result = total[:16]
    pieces = [send(low[16 * k - 16 : 16 * k], source=lambda c, h, k=k: (c, (h - 2 * k) % 8)) for k in (1, 3, 2)]
    for piece in pieces:
        result = result + piece.astype(F32)
    return (
        dq.reshape(tokens, heads, width),
        dqr.reshape(tokens, heads, ROPE),
        result[:, :512],
        result[:, 512 : 512 + ROPE],
    )


def solution(mesh):
    in_specs = (
        P("ctx", "hg", None), P("ctx", "hg", None), P("ctx", None), P("ctx", None), P("ctx", "hg", None), P(),
    )
    out_specs = (P("ctx", "hg", None), P("ctx", "hg", None), P(("ctx", "hg"), None), P(("ctx", "hg"), None))
    return jax.shard_map(on_device, mesh=mesh, in_specs=in_specs, out_specs=out_specs, check_vma=False)
```

```python
import functools

import jax
import jax.numpy as jnp
from jax import lax
from jax.experimental import pallas as pl
from jax.experimental.pallas import tpu as pltpu
from jax.sharding import PartitionSpec as P

SCALE = 192.0 ** (-0.5)
LOG2E = 1.4426950408889634
F32, BF16 = jnp.float32, jnp.bfloat16
TOK = 128
ROPE = 64
WIDE = 640
VM = pltpu.VMEM


def moved(block, sizes, source):
    n_c, n_h = sizes
    route = []
    for c in range(n_c):
        for h in range(n_h):
            sc, sh = source(c, h)
            route.append(((sc % n_c) * n_h + sh % n_h, c * n_h + h))
    return lax.ppermute(block, ("ctx", "hg"), route)


def far_source(c):
    return c - 1 if c % 2 else c - 3


def far_home(c):
    return c + 3 if c % 2 else c + 1


def slot_cycles(me, n):
    odd = lax.rem(me, 2)
    far = me - 3 + 2 * odd
    swp = me - 1 - 2 * odd
    return [lax.rem(x + n, n) for x in (me, me - 2, far, swp)]


def pack_kernel(nope, rope_t, out):
    out[0:TOK, :] = nope[...]
    for j in range(4):
        out[TOK : TOK + 16, 128 * j : 128 * j + 128] = rope_t[16 * j : 16 * j + 16, :]


def unpack(ref, kcat, kr, at):
    kcat[at : at + TOK, :] = ref[0:TOK, :]
    rope_t = jnp.concatenate(
        [ref[TOK : TOK + 16, 128 * j : 128 * j + 128].astype(F32) for j in range(4)], axis=0
    )
    kr[at : at + TOK, :] = rope_t.T.astype(BF16)


def products(k, kr, q, qr, do):
    nt = (((1,), (1,)), ((), ()))
    s_t = lax.dot_general(k, q, nt, preferred_element_type=F32)
    s_t += lax.dot_general(kr, qr, nt, preferred_element_type=F32)
    return s_t, lax.dot_general(k, do, nt, preferred_element_type=F32)


def fetch_kernel(q, do, q_out, do_out):
    rb = q.shape[0]
    at = pl.ds(pl.multiple_of(pl.program_id(0) * rb, rb), rb)
    q_out[at, :] = q[...]
    do_out[at, :] = do[...]


def local_kernel(rb, q, qr, do, own, s_own, d_own, kcat, kr):
    unpack(own, kcat, kr, 0)
    for i in range(q.shape[0] // rb):
        at = slice(i * rb, i * rb + rb)
        s_own[:, at], d_own[:, at] = products(kcat[...], kr[...], q[at, :], qr[at, :], do[at, :])


def finish_kernel(own, one, three, two, nope, rope):
    total = own[...] + one[...].astype(F32) + three[...].astype(F32) + two[...].astype(F32)
    nope[...] = total[:, 0:512]
    rope[...] = total[:, 512 : 512 + ROPE]


def score_kernel(n_ctx, rb, mask, q, qr, do, s_own, d_own, own, two, far, swp, dst, pt, kcat, kr):
    for s, ref in enumerate((own, two, far, swp)):
        unpack(ref, kcat, kr, TOK * s)
    cycles = slot_cycles(lax.axis_index("ctx"), n_ctx)
    steps = q.shape[0] // rb
    for i in range(steps):
        at = slice(i * rb, i * rb + rb)
        s_t, d_t = products(kcat[TOK:, :], kr[TOK:, :], q[at, :], qr[at, :], do[at, :])
        s_t = jnp.concatenate([s_own[:, at], s_t], axis=0)
        d_t = jnp.concatenate([d_own[:, at], d_t], axis=0)
        half = 2 * i // steps
        parts = []
        for b in range(8):
            bias = jnp.where(mask[half, 2 * cycles[b // 2] + b % 2] == 1, 0.0, -1e30).astype(F32)
            parts.append(s_t[64 * b : 64 * b + 64, :] * (SCALE * LOG2E) + bias)
        s_t = jnp.concatenate(parts, axis=0)
        e = jnp.exp2(s_t - jnp.max(s_t, axis=0, keepdims=True))
        inv = 1.0 / jnp.sum(e, axis=0, keepdims=True)
        delta = jnp.sum(e * d_t, axis=0, keepdims=True) * inv
        p = e * inv
        dst[:, at] = (p * ((d_t - delta) * SCALE)).astype(BF16)
        pt[:, at] = p.astype(BF16)


def latent_kernel(first, rb, dst, pt, q, qr, do, *rest):
    *outs, acc, accr = rest
    me_h = lax.axis_index("hg")
    keys = slice(first, first + 2 * TOK)
    total, total_r = None, None
    for i in range(q.shape[0] // rb):
        at = slice(i * rb, i * rb + rb)
        part = jnp.dot(dst[keys, at], q[at, :], preferred_element_type=F32) + jnp.dot(
            pt[keys, at], do[at, :], preferred_element_type=F32
        )
        part_r = jnp.dot(dst[keys, at], qr[at, :], preferred_element_type=F32)
        total = part if total is None else total + part
        total_r = part_r if total_r is None else total_r + part_r
    acc[...] = total
    accr[...] = total_r
    me_x, me_y = me_h // 2, lax.rem(me_h, 2)
    for slot, out in enumerate(outs):
        for other in range(2):
            y = me_y if other == 0 else 1 - me_y
            for k in range(4):
                x = lax.rem(me_x + k, 4)
                row = pl.multiple_of(TOK * slot + (2 * x + y) * 16, 16)
                to = 64 * other + 16 * k
                out[to : to + 16, 0:512] = acc[pl.ds(row, 16), :].astype(out.dtype)
                out[to : to + 16, 512 : 512 + ROPE] = accr[pl.ds(row, 16), :].astype(out.dtype)
                out[to : to + 16, 512 + ROPE : WIDE] = jnp.zeros((16, WIDE - 512 - ROPE), out.dtype)


def dq_kernel(dst, kcat, kr, dq, dqr):
    tn = (((0,), (0,)), ((), ()))
    rb = dq.shape[0]
    at = pl.ds(pl.multiple_of(pl.program_id(0) * rb, rb), rb)
    dq[...] = lax.dot_general(dst[:, at], kcat[...], tn, preferred_element_type=F32).astype(BF16)
    dqr[...] = lax.dot_general(dst[:, at], kr[...], tn, preferred_element_type=F32).astype(BF16)


def whole(shape):
    return pl.BlockSpec(shape, lambda i: (0,) * len(shape), pipeline_mode=pl.Buffered(1))


HERE = pl.BlockSpec(memory_space=VM)
ROWS = 512


def arrays(*pairs):
    return [jax.ShapeDtypeStruct(s, t) for s, t in pairs]


def fetched(q, do):
    rows, width = q.shape
    block = pl.BlockSpec((ROWS, width), lambda i: (i, 0))
    return pl.pallas_call(
        fetch_kernel,
        name="fetched",
        grid=(rows // ROWS,),
        in_specs=[block, block],
        out_specs=[HERE] * 2,
        out_shape=arrays(((rows, width), BF16), ((rows, width), BF16)),
        compiler_params=pltpu.CompilerParams(vmem_limit_bytes=24 << 20),
        cost_estimate=pl.CostEstimate(flops=1000, bytes_accessed=8_000_000, transcendentals=0),
    )(pltpu.with_memory_space_constraint(q, pltpu.HBM), pltpu.with_memory_space_constraint(do, pltpu.HBM))


def local_scores(q, qr, do, own):
    rows, width = q.shape
    return pl.pallas_call(
        functools.partial(local_kernel, ROWS),
        name="local_scores",
        in_specs=[HERE] * 4,
        out_specs=[HERE] * 2,
        out_shape=arrays(((TOK, rows), F32), ((TOK, rows), F32)),
        scratch_shapes=[VM((TOK, width), BF16), VM((TOK, ROPE), BF16)],
        compiler_params=pltpu.CompilerParams(vmem_limit_bytes=24 << 20),
        cost_estimate=pl.CostEstimate(flops=600_000_000, bytes_accessed=5_000_000, transcendentals=0),
    )(q, qr, do, own)


def scores(n_ctx, mask, q, qr, do, s_own, d_own, slots):
    rows, width = q.shape
    keys = 4 * TOK
    return pl.pallas_call(
        functools.partial(score_kernel, n_ctx, ROWS),
        name="scores",
        in_specs=[pl.BlockSpec(memory_space=pltpu.SMEM)] + [HERE] * 9,
        out_specs=[HERE] * 4,
        out_shape=arrays(((keys, rows), BF16), ((keys, rows), BF16), ((keys, width), BF16), ((keys, ROPE), BF16)),
        compiler_params=pltpu.CompilerParams(vmem_limit_bytes=28 << 20),
        cost_estimate=pl.CostEstimate(flops=1_800_000_000, bytes_accessed=9_000_000, transcendentals=1 << 20),
    )(mask, q, qr, do, s_own, d_own, *slots)


def latent_gradient(which, name, dst, pt, q, qr, do, types):
    rows, width = q.shape
    return pl.pallas_call(
        functools.partial(latent_kernel, 2 * TOK * which, 1024),
        name=name,
        in_specs=[HERE] * 5,
        out_specs=[HERE] * 2,
        out_shape=arrays(*[((TOK, WIDE), t) for t in types]),
        scratch_shapes=[VM((2 * TOK, width), F32), VM((2 * TOK, ROPE), F32)],
        compiler_params=pltpu.CompilerParams(vmem_limit_bytes=24 << 20),
        cost_estimate=pl.CostEstimate(flops=1_200_000_000, bytes_accessed=6_000_000, transcendentals=0),
    )(dst, pt, q, qr, do)


def query_gradient(dst, kcat, kr):
    keys, rows = dst.shape
    width = kcat.shape[1]
    return pl.pallas_call(
        dq_kernel,
        name="query_gradient",
        grid=(rows // ROWS,),
        in_specs=[HERE] * 3,
        out_specs=[
            pl.BlockSpec((ROWS, width), lambda i: (i, 0)), pl.BlockSpec((ROWS, ROPE), lambda i: (i, 0)),
        ],
        out_shape=arrays(((rows, width), BF16), ((rows, ROPE), BF16)),
        compiler_params=pltpu.CompilerParams(vmem_limit_bytes=16 << 20),
        cost_estimate=pl.CostEstimate(flops=2_400_000_000, bytes_accessed=5_000_000, transcendentals=0),
    )(dst, kcat, kr)


def on_device(query_latent_plain, query_rope, latent_nope, latent_rope, latent_output_gradient, block_mask):
    tokens, heads, width = query_latent_plain.shape
    rows = tokens * heads
    sizes = (lax.axis_size("ctx"), lax.axis_size("hg"))
    send = functools.partial(moved, sizes=sizes)
    own = pl.pallas_call(
        pack_kernel, name="pack", out_shape=jax.ShapeDtypeStruct((TOK + 16, width), BF16)
    )(latent_nope, latent_rope.T)
    two = send(own, source=lambda c, h: (c - 2, h))
    far = send(own, source=lambda c, h: (far_source(c), h))
    mask = lax.dynamic_slice(block_mask, (2 * lax.axis_index("ctx"), 0), (2, block_mask.shape[1]))
    qr = query_rope.reshape(rows, ROPE)
    qr, mask, query_latent_plain, latent_output_gradient = lax.optimization_barrier(
        (qr, mask, query_latent_plain, latent_output_gradient)
    )
    q, do = fetched(query_latent_plain.reshape(rows, width), latent_output_gradient.reshape(rows, width))
    two, q, do, qr = lax.optimization_barrier((two, q, do, qr))
    swp = send(two, source=lambda c, h: (c ^ 1, h))
    s_own, d_own = local_scores(q, qr, do, own)
    s_own, d_own, swp, far = lax.optimization_barrier((s_own, d_own, swp, far))
    dst, pt, kcat, kr = scores(sizes[0], mask, q, qr, do, s_own, d_own, (own, two, far, swp))
    far_dk, swp_dk = latent_gradient(1, "latent_far", dst, pt, q, qr, do, (BF16, BF16))
    got_swp = send(swp_dk, source=lambda c, h: (c ^ 1, h))
    got_far = send(far_dk, source=lambda c, h: (far_home(c), h))
    dst, pt, swp_dk, far_dk = lax.optimization_barrier((dst, pt, swp_dk, far_dk))
    own_dk, two_dk = latent_gradient(0, "latent_near", dst, pt, q, qr, do, (F32, F32))
    two_dk, got_swp = lax.optimization_barrier((two_dk, got_swp))
    two_same = (two_dk[:64] + got_swp[:64].astype(F32)).astype(BF16)
    two_other = (two_dk[64:] + got_swp[64:].astype(F32)).astype(BF16)
    got_two = send(two_same, source=lambda c, h: (c + 2, h))
    got_two_y = send(two_other, source=lambda c, h: (c + 2, h ^ 1))
    own_other = (own_dk[64:] + got_far[64:].astype(F32)).astype(BF16)
    got_own_y = send(own_other, source=lambda c, h: (c, h ^ 1))
    dst, two_same, two_other, own_other = lax.optimization_barrier((dst, two_same, two_other, own_other))
    dq, dqr = query_gradient(dst, kcat, kr)
    dq, dqr, got_two, got_two_y, got_own_y = lax.optimization_barrier((dq, dqr, got_two, got_two_y, got_own_y))
    total = own_dk[:64] + got_far[:64].astype(F32)
    for got in (got_own_y, got_two, got_two_y):
        total = total + got.astype(F32)
    low = total[16:].astype(BF16)
    pieces = [send(low[16 * k - 16 : 16 * k], source=lambda c, h, k=k: (c, (h - 2 * k) % 8)) for k in (1, 3, 2)]
    nope, rope = pl.pallas_call(
        finish_kernel,
        name="finish",
        out_shape=[jax.ShapeDtypeStruct((16, width), F32), jax.ShapeDtypeStruct((16, ROPE), F32)],
        compiler_params=pltpu.CompilerParams(vmem_limit_bytes=2 << 20),
    )(total[:16], *pieces)
    return (dq.reshape(tokens, heads, width), dqr.reshape(tokens, heads, ROPE), nope, rope)


def solution(mesh):
    in_specs = (
        P("ctx", "hg", None), P("ctx", "hg", None), P("ctx", None), P("ctx", None), P("ctx", "hg", None), P(),
    )
    out_specs = (P("ctx", "hg", None), P("ctx", "hg", None), P(("ctx", "hg"), None), P(("ctx", "hg"), None))
    return jax.shard_map(on_device, mesh=mesh, in_specs=in_specs, out_specs=out_specs, check_vma=False)
```

```python
import functools

import jax
import jax.numpy as jnp
from jax import lax
from jax.experimental import pallas as pl
from jax.experimental.pallas import tpu as pltpu
from jax.sharding import PartitionSpec as P

SCALE = 192.0 ** (-0.5)
LOG2E = 1.4426950408889634
F32, BF16 = jnp.float32, jnp.bfloat16
TOK = 128
ROPE = 64
WIDE = 640
VM = pltpu.VMEM


def moved(block, sizes, source):
    n_c, n_h = sizes
    route = []
    for c in range(n_c):
        for h in range(n_h):
            sc, sh = source(c, h)
            route.append(((sc % n_c) * n_h + sh % n_h, c * n_h + h))
    return lax.ppermute(block, ("ctx", "hg"), route)


def far_source(c):
    return c - 1 if c % 2 else c - 3


def far_home(c):
    return c + 3 if c % 2 else c + 1


def slot_cycles(me, n):
    odd = lax.rem(me, 2)
    far = me - 3 + 2 * odd
    swp = me - 1 - 2 * odd
    return [lax.rem(x + n, n) for x in (me, me - 2, far, swp)]


def pack_kernel(nope, rope_t, out):
    out[0:TOK, :] = nope[...]
    for j in range(4):
        out[TOK : TOK + 16, 128 * j : 128 * j + 128] = rope_t[16 * j : 16 * j + 16, :]


def unpack(ref, kcat, kr, at):
    kcat[at : at + TOK, :] = ref[0:TOK, :]
    rope_t = jnp.concatenate(
        [ref[TOK : TOK + 16, 128 * j : 128 * j + 128].astype(F32) for j in range(4)], axis=0
    )
    kr[at : at + TOK, :] = rope_t.T.astype(BF16)


def products(k, kr, q, qr, do):
    nt = (((1,), (1,)), ((), ()))
    s_t = lax.dot_general(k, q, nt, preferred_element_type=F32)
    s_t += lax.dot_general(kr, qr, nt, preferred_element_type=F32)
    return s_t, lax.dot_general(k, do, nt, preferred_element_type=F32)


def local_kernel(rb, q, do, rope, own, q_out, do_out, qr, s_own, d_own, kcat, kr, rope_in, turned, sems):
    copies = []
    rope_copy = pltpu.make_async_copy(rope, rope_in, sems.at[2 * (q.shape[0] // rb)])
    rope_copy.start()
    for i in range(q.shape[0] // rb):
        at = pl.ds(i * rb, rb)
        copies.append(pltpu.make_async_copy(q.at[at, :], q_out.at[at, :], sems.at[2 * i]))
        copies.append(pltpu.make_async_copy(do.at[at, :], do_out.at[at, :], sems.at[2 * i + 1]))
    for copy in copies:
        copy.start()
    unpack(own, kcat, kr, 0)
    heads, _, tokens = rope.shape
    rope_copy.wait()
    for h in range(heads):
        turned[pl.ds(h, tokens, stride=heads), :] = rope_in[h].astype(F32).T
    qr[...] = turned[...].astype(BF16)
    for i in range(q.shape[0] // rb):
        at = slice(i * rb, i * rb + rb)
        copies[2 * i].wait()
        copies[2 * i + 1].wait()
        s_own[:, at], d_own[:, at] = products(kcat[...], kr[...], q_out[at, :], qr[at, :], do_out[at, :])


def finish_kernel(own, one, three, two, nope, rope):
    total = own[...] + one[...].astype(F32) + three[...].astype(F32) + two[...].astype(F32)
    nope[...] = total[:, 0:512]
    rope[...] = total[:, 512 : 512 + ROPE]


def score_kernel(n_ctx, rb, mask, q, qr, do, s_own, d_own, own, two, far, swp, dst, pt, kcat, kr):
    for s, ref in enumerate((own, two, far, swp)):
        unpack(ref, kcat, kr, TOK * s)
    cycles = slot_cycles(lax.axis_index("ctx"), n_ctx)
    steps = q.shape[0] // rb
    for i in range(steps):
        at = slice(i * rb, i * rb + rb)
        s_t, d_t = products(kcat[TOK:, :], kr[TOK:, :], q[at, :], qr[at, :], do[at, :])
        s_t = jnp.concatenate([s_own[:, at], s_t], axis=0)
        d_t = jnp.concatenate([d_own[:, at], d_t], axis=0)
        half = 2 * i // steps
        parts = []
        for b in range(8):
            bias = jnp.where(mask[half, 2 * cycles[b // 2] + b % 2] == 1, 0.0, -1e30).astype(F32)
            parts.append(s_t[64 * b : 64 * b + 64, :] * (SCALE * LOG2E) + bias)
        s_t = jnp.concatenate(parts, axis=0)
        e = jnp.exp2(s_t - jnp.max(s_t, axis=0, keepdims=True))
        inv = 1.0 / jnp.sum(e, axis=0, keepdims=True)
        delta = jnp.sum(e * d_t, axis=0, keepdims=True) * inv
        p = e * inv
        dst[:, at] = (p * ((d_t - delta) * SCALE)).astype(BF16)
        pt[:, at] = p.astype(BF16)


def latent_kernel(first, rb, dst, pt, q, qr, do, *rest):
    *outs, acc, accr = rest
    me_h = lax.axis_index("hg")
    keys = slice(first, first + 2 * TOK)
    total, total_r = None, None
    for i in range(q.shape[0] // rb):
        at = slice(i * rb, i * rb + rb)
        part = jnp.dot(dst[keys, at], q[at, :], preferred_element_type=F32) + jnp.dot(
            pt[keys, at], do[at, :], preferred_element_type=F32
        )
        part_r = jnp.dot(dst[keys, at], qr[at, :], preferred_element_type=F32)
        total = part if total is None else total + part
        total_r = part_r if total_r is None else total_r + part_r
    acc[...] = total
    accr[...] = total_r
    me_x, me_y = me_h // 2, lax.rem(me_h, 2)
    for slot, out in enumerate(outs):
        for other in range(2):
            y = me_y if other == 0 else 1 - me_y
            for k in range(4):
                x = lax.rem(me_x + k, 4)
                row = pl.multiple_of(TOK * slot + (2 * x + y) * 16, 16)
                to = 64 * other + 16 * k
                out[to : to + 16, 0:512] = acc[pl.ds(row, 16), :].astype(out.dtype)
                out[to : to + 16, 512 : 512 + ROPE] = accr[pl.ds(row, 16), :].astype(out.dtype)
                out[to : to + 16, 512 + ROPE : WIDE] = jnp.zeros((16, WIDE - 512 - ROPE), out.dtype)


def dq_kernel(dst, kcat, kr, dq, dqr):
    tn = (((0,), (0,)), ((), ()))
    rb = dq.shape[0]
    at = pl.ds(pl.multiple_of(pl.program_id(0) * rb, rb), rb)
    dq[...] = lax.dot_general(dst[:, at], kcat[...], tn, preferred_element_type=F32).astype(BF16)
    dqr[...] = lax.dot_general(dst[:, at], kr[...], tn, preferred_element_type=F32).astype(BF16)


def whole(shape):
    return pl.BlockSpec(shape, lambda i: (0,) * len(shape), pipeline_mode=pl.Buffered(1))


HERE = pl.BlockSpec(memory_space=VM)
ROWS = 512


def arrays(*pairs):
    return [jax.ShapeDtypeStruct(s, t) for s, t in pairs]


def local_scores(q, do, rope, own):
    rows, width = q.shape
    hbm = pl.BlockSpec(memory_space=pl.ANY)
    return pl.pallas_call(
        functools.partial(local_kernel, ROWS),
        name="local_scores",
        in_specs=[hbm, hbm, hbm, HERE],
        out_specs=[HERE] * 5,
        out_shape=arrays(
            ((rows, width), BF16), ((rows, width), BF16), ((rows, ROPE), BF16), ((TOK, rows), F32), ((TOK, rows), F32)
        ),
        scratch_shapes=[
            VM((TOK, width), BF16), VM((TOK, ROPE), BF16), VM(rope.shape, BF16), VM((rows, ROPE), F32),
            pltpu.SemaphoreType.DMA((2 * rows // ROWS + 1,)),
        ],
        compiler_params=pltpu.CompilerParams(vmem_limit_bytes=16 << 20),
        cost_estimate=pl.CostEstimate(flops=600_000_000, bytes_accessed=8_000_000, transcendentals=0),
    )(*(pltpu.with_memory_space_constraint(a, pltpu.HBM) for a in (q, do, rope)), own)


def scores(n_ctx, mask, q, qr, do, s_own, d_own, slots):
    rows, width = q.shape
    keys = 4 * TOK
    return pl.pallas_call(
        functools.partial(score_kernel, n_ctx, ROWS),
        name="scores",
        in_specs=[pl.BlockSpec(memory_space=pltpu.SMEM)] + [HERE] * 9,
        out_specs=[HERE] * 4,
        out_shape=arrays(((keys, rows), BF16), ((keys, rows), BF16), ((keys, width), BF16), ((keys, ROPE), BF16)),
        compiler_params=pltpu.CompilerParams(vmem_limit_bytes=28 << 20),
        cost_estimate=pl.CostEstimate(flops=1_800_000_000, bytes_accessed=9_000_000, transcendentals=1 << 20),
    )(mask, q, qr, do, s_own, d_own, *slots)


def latent_gradient(which, name, dst, pt, q, qr, do, types):
    rows, width = q.shape
    return pl.pallas_call(
        functools.partial(latent_kernel, 2 * TOK * which, 1024),
        name=name,
        in_specs=[HERE] * 5,
        out_specs=[HERE] * 2,
        out_shape=arrays(*[((TOK, WIDE), t) for t in types]),
        scratch_shapes=[VM((2 * TOK, width), F32), VM((2 * TOK, ROPE), F32)],
        compiler_params=pltpu.CompilerParams(vmem_limit_bytes=24 << 20),
        cost_estimate=pl.CostEstimate(flops=1_200_000_000, bytes_accessed=6_000_000, transcendentals=0),
    )(dst, pt, q, qr, do)


def query_gradient(dst, kcat, kr):
    keys, rows = dst.shape
    width = kcat.shape[1]
    return pl.pallas_call(
        dq_kernel,
        name="query_gradient",
        grid=(rows // ROWS,),
        in_specs=[HERE] * 3,
        out_specs=[
            pl.BlockSpec((ROWS, width), lambda i: (i, 0)), pl.BlockSpec((ROWS, ROPE), lambda i: (i, 0)),
        ],
        out_shape=arrays(((rows, width), BF16), ((rows, ROPE), BF16)),
        compiler_params=pltpu.CompilerParams(vmem_limit_bytes=16 << 20),
        cost_estimate=pl.CostEstimate(flops=2_400_000_000, bytes_accessed=5_000_000, transcendentals=0),
    )(dst, kcat, kr)


def on_device(query_latent_plain, query_rope, latent_nope, latent_rope, latent_output_gradient, block_mask):
    tokens, heads, width = query_latent_plain.shape
    rows = tokens * heads
    sizes = (lax.axis_size("ctx"), lax.axis_size("hg"))
    send = functools.partial(moved, sizes=sizes)
    own = pl.pallas_call(
        pack_kernel,
        name="pack",
        in_specs=[pl.BlockSpec((TOK, width), lambda: (0, 0)), pl.BlockSpec((ROPE, TOK), lambda: (0, 0))],
        out_specs=HERE,
        out_shape=jax.ShapeDtypeStruct((TOK + 16, width), BF16),
        compiler_params=pltpu.CompilerParams(vmem_limit_bytes=4 << 20),
    )(
        pltpu.with_memory_space_constraint(latent_nope, pltpu.HBM),
        pltpu.with_memory_space_constraint(latent_rope.T, pltpu.HBM),
    )
    two = send(own, source=lambda c, h: (c - 2, h))
    mask = lax.dynamic_slice(block_mask, (2 * lax.axis_index("ctx"), 0), (2, block_mask.shape[1]))
    mask, own_far, query_latent_plain, latent_output_gradient = lax.optimization_barrier(
        (mask, own, query_latent_plain, latent_output_gradient)
    )
    far = send(own_far, source=lambda c, h: (far_source(c), h))
    q, do, qr, s_own, d_own = local_scores(
        query_latent_plain.reshape(rows, width),
        latent_output_gradient.reshape(rows, width),
        jnp.transpose(query_rope, (1, 2, 0)),
        own,
    )
    two, q, do, s_own, d_own, qr = lax.optimization_barrier((two, q, do, s_own, d_own, qr))
    swp = send(two, source=lambda c, h: (c ^ 1, h))
    swp, far = lax.optimization_barrier((swp, far))
    dst, pt, kcat, kr = scores(sizes[0], mask, q, qr, do, s_own, d_own, (own, two, far, swp))
    far_dk, swp_dk = latent_gradient(1, "latent_far", dst, pt, q, qr, do, (BF16, BF16))
    got_swp = send(swp_dk, source=lambda c, h: (c ^ 1, h))
    got_far = send(far_dk, source=lambda c, h: (far_home(c), h))
    dst, pt, swp_dk, far_dk = lax.optimization_barrier((dst, pt, swp_dk, far_dk))
    own_dk, two_dk = latent_gradient(0, "latent_near", dst, pt, q, qr, do, (F32, F32))
    two_dk, got_swp = lax.optimization_barrier((two_dk, got_swp))
    two_same = (two_dk[:64] + got_swp[:64].astype(F32)).astype(BF16)
    two_other = (two_dk[64:] + got_swp[64:].astype(F32)).astype(BF16)
    got_two = send(two_same, source=lambda c, h: (c + 2, h))
    got_two_y = send(two_other, source=lambda c, h: (c + 2, h ^ 1))
    own_other = (own_dk[64:] + got_far[64:].astype(F32)).astype(BF16)
    got_own_y = send(own_other, source=lambda c, h: (c, h ^ 1))
    dst, two_same, two_other, own_other = lax.optimization_barrier((dst, two_same, two_other, own_other))
    dq, dqr = query_gradient(dst, kcat, kr)
    dq, dqr, got_two, got_two_y, got_own_y = lax.optimization_barrier((dq, dqr, got_two, got_two_y, got_own_y))
    total = own_dk[:64] + got_far[:64].astype(F32)
    for got in (got_own_y, got_two, got_two_y):
        total = total + got.astype(F32)
    low = total[16:].astype(BF16)
    pieces = [send(low[16 * k - 16 : 16 * k], source=lambda c, h, k=k: (c, (h - 2 * k) % 8)) for k in (1, 3, 2)]
    nope, rope = pl.pallas_call(
        finish_kernel,
        name="finish",
        out_shape=[jax.ShapeDtypeStruct((16, width), F32), jax.ShapeDtypeStruct((16, ROPE), F32)],
        compiler_params=pltpu.CompilerParams(vmem_limit_bytes=2 << 20),
    )(total[:16], *pieces)
    return (dq.reshape(tokens, heads, width), dqr.reshape(tokens, heads, ROPE), nope, rope)


def solution(mesh):
    in_specs = (
        P("ctx", "hg", None), P("ctx", "hg", None), P("ctx", None), P("ctx", None), P("ctx", "hg", None), P(),
    )
    out_specs = (P("ctx", "hg", None), P("ctx", "hg", None), P(("ctx", "hg"), None), P(("ctx", "hg"), None))
    return jax.shard_map(on_device, mesh=mesh, in_specs=in_specs, out_specs=out_specs, check_vma=False)
```

```python
import functools

import jax
import jax.numpy as jnp
from jax import lax
from jax.experimental import pallas as pl
from jax.experimental.pallas import tpu as pltpu
from jax.sharding import PartitionSpec as P

SCALE = 192.0 ** (-0.5)
LOG2E = 1.4426950408889634
F32, BF16 = jnp.float32, jnp.bfloat16
TOK = 128
ROPE = 64
WIDE = 640
VM = pltpu.VMEM


def moved(block, sizes, source):
    n_c, n_h = sizes
    route = []
    for c in range(n_c):
        for h in range(n_h):
            sc, sh = source(c, h)
            route.append(((sc % n_c) * n_h + sh % n_h, c * n_h + h))
    return lax.ppermute(block, ("ctx", "hg"), route)


def far_source(c):
    return c - 1 if c % 2 else c - 3


def far_home(c):
    return c + 3 if c % 2 else c + 1


def slot_cycles(me, n):
    odd = lax.rem(me, 2)
    far = me - 3 + 2 * odd
    swp = me - 1 - 2 * odd
    return [lax.rem(x + n, n) for x in (me, me - 2, far, swp)]


def pack_kernel(nope, rope_t, out):
    out[0:TOK, :] = nope[...]
    for j in range(4):
        out[TOK : TOK + 16, 128 * j : 128 * j + 128] = rope_t[16 * j : 16 * j + 16, :]


def unpack(ref, kcat, kr, at):
    kcat[at : at + TOK, :] = ref[0:TOK, :]
    rope_t = jnp.concatenate(
        [ref[TOK : TOK + 16, 128 * j : 128 * j + 128].astype(F32) for j in range(4)], axis=0
    )
    kr[at : at + TOK, :] = rope_t.T.astype(BF16)


def products(k, kr, q, qr, do):
    nt = (((1,), (1,)), ((), ()))
    s_t = lax.dot_general(k, q, nt, preferred_element_type=F32)
    s_t += lax.dot_general(kr, qr, nt, preferred_element_type=F32)
    return s_t, lax.dot_general(k, do, nt, preferred_element_type=F32)


def local_kernel(rb, q, do, rope, own, q_out, do_out, qr, s_own, d_own, kcat, kr, rope_in, turned, sems):
    copies = []
    rope_copy = pltpu.make_async_copy(rope, rope_in, sems.at[2 * (q.shape[0] // rb)])
    rope_copy.start()
    for i in range(q.shape[0] // rb):
        at = pl.ds(i * rb, rb)
        copies.append(pltpu.make_async_copy(q.at[at, :], q_out.at[at, :], sems.at[2 * i]))
        copies.append(pltpu.make_async_copy(do.at[at, :], do_out.at[at, :], sems.at[2 * i + 1]))
    for copy in copies:
        copy.start()
    unpack(own, kcat, kr, 0)
    heads, _, tokens = rope.shape
    rope_copy.wait()
    for h in range(heads):
        turned[pl.ds(h, tokens, stride=heads), :] = rope_in[h].astype(F32).T
    qr[...] = turned[...].astype(BF16)
    for i in range(q.shape[0] // rb):
        at = slice(i * rb, i * rb + rb)
        copies[2 * i].wait()
        copies[2 * i + 1].wait()
        s_own[:, at], d_own[:, at] = products(kcat[...], kr[...], q_out[at, :], qr[at, :], do_out[at, :])


def finish_kernel(own, one, three, two, nope, rope):
    total = own[...] + one[...].astype(F32) + three[...].astype(F32) + two[...].astype(F32)
    nope[...] = total[:, 0:512]
    rope[...] = total[:, 512 : 512 + ROPE]


def score_kernel(n_ctx, rb, mask, q, qr, do, s_own, d_own, own, two, far, swp, dst, pt, kcat, kr):
    for s, ref in enumerate((own, two, far, swp)):
        unpack(ref, kcat, kr, TOK * s)
    cycles = slot_cycles(lax.axis_index("ctx"), n_ctx)
    steps = q.shape[0] // rb
    for i in range(steps):
        at = slice(i * rb, i * rb + rb)
        s_t, d_t = products(kcat[TOK:, :], kr[TOK:, :], q[at, :], qr[at, :], do[at, :])
        s_t = jnp.concatenate([s_own[:, at], s_t], axis=0)
        d_t = jnp.concatenate([d_own[:, at], d_t], axis=0)
        half = 2 * i // steps
        parts = []
        for b in range(8):
            bias = jnp.where(mask[half, 2 * cycles[b // 2] + b % 2] == 1, 0.0, -1e30).astype(F32)
            parts.append(s_t[64 * b : 64 * b + 64, :] * (SCALE * LOG2E) + bias)
        s_t = jnp.concatenate(parts, axis=0)
        e = jnp.exp2(s_t - jnp.max(s_t, axis=0, keepdims=True))
        inv = 1.0 / jnp.sum(e, axis=0, keepdims=True)
        delta = jnp.sum(e * d_t, axis=0, keepdims=True) * inv
        p = e * inv
        dst[:, at] = (p * ((d_t - delta) * SCALE)).astype(BF16)
        pt[:, at] = p.astype(BF16)


def latent_kernel(first, rb, dst, pt, q, qr, do, *rest):
    *outs, acc, accr = rest
    me_h = lax.axis_index("hg")
    keys = slice(first, first + 2 * TOK)
    total, total_r = None, None
    for i in range(q.shape[0] // rb):
        at = slice(i * rb, i * rb + rb)
        part = jnp.dot(dst[keys, at], q[at, :], preferred_element_type=F32) + jnp.dot(
            pt[keys, at], do[at, :], preferred_element_type=F32
        )
        part_r = jnp.dot(dst[keys, at], qr[at, :], preferred_element_type=F32)
        total = part if total is None else total + part
        total_r = part_r if total_r is None else total_r + part_r
    acc[...] = total
    accr[...] = total_r
    me_x, me_y = me_h // 2, lax.rem(me_h, 2)
    for slot, out in enumerate(outs):
        for other in range(2):
            y = me_y if other == 0 else 1 - me_y
            for k in range(4):
                x = lax.rem(me_x + k, 4)
                row = pl.multiple_of(TOK * slot + (2 * x + y) * 16, 16)
                to = 64 * other + 16 * k
                out[to : to + 16, 0:512] = acc[pl.ds(row, 16), :].astype(out.dtype)
                out[to : to + 16, 512 : 512 + ROPE] = accr[pl.ds(row, 16), :].astype(out.dtype)
                out[to : to + 16, 512 + ROPE : WIDE] = jnp.zeros((16, WIDE - 512 - ROPE), out.dtype)


def dq_kernel(dst, kcat, kr, dq, dqr):
    tn = (((0,), (0,)), ((), ()))
    rb = dq.shape[0]
    at = pl.ds(pl.multiple_of(pl.program_id(0) * rb, rb), rb)
    dq[...] = lax.dot_general(dst[:, at], kcat[...], tn, preferred_element_type=F32).astype(BF16)
    dqr[...] = lax.dot_general(dst[:, at], kr[...], tn, preferred_element_type=F32).astype(BF16)


def whole(shape):
    return pl.BlockSpec(shape, lambda i: (0,) * len(shape), pipeline_mode=pl.Buffered(1))


HERE = pl.BlockSpec(memory_space=VM)
ROWS = 512


def arrays(*pairs):
    return [jax.ShapeDtypeStruct(s, t) for s, t in pairs]


def local_scores(q, do, rope, own):
    rows, width = q.shape
    hbm = pl.BlockSpec(memory_space=pl.ANY)
    return pl.pallas_call(
        functools.partial(local_kernel, ROWS),
        name="local_scores",
        in_specs=[hbm, hbm, hbm, HERE],
        out_specs=[HERE] * 5,
        out_shape=arrays(
            ((rows, width), BF16), ((rows, width), BF16), ((rows, ROPE), BF16), ((TOK, rows), F32), ((TOK, rows), F32)
        ),
        scratch_shapes=[
            VM((TOK, width), BF16), VM((TOK, ROPE), BF16), VM(rope.shape, BF16), VM((rows, ROPE), F32),
            pltpu.SemaphoreType.DMA((2 * rows // ROWS + 1,)),
        ],
        compiler_params=pltpu.CompilerParams(vmem_limit_bytes=16 << 20),
        cost_estimate=pl.CostEstimate(flops=600_000_000, bytes_accessed=8_000_000, transcendentals=0),
    )(*(pltpu.with_memory_space_constraint(a, pltpu.HBM) for a in (q, do, rope)), own)


def scores(n_ctx, mask, q, qr, do, s_own, d_own, slots):
    rows, width = q.shape
    keys = 4 * TOK
    return pl.pallas_call(
        functools.partial(score_kernel, n_ctx, ROWS),
        name="scores",
        in_specs=[pl.BlockSpec(memory_space=pltpu.SMEM)] + [HERE] * 9,
        out_specs=[HERE] * 4,
        out_shape=arrays(((keys, rows), BF16), ((keys, rows), BF16), ((keys, width), BF16), ((keys, ROPE), BF16)),
        compiler_params=pltpu.CompilerParams(vmem_limit_bytes=28 << 20),
        cost_estimate=pl.CostEstimate(flops=1_800_000_000, bytes_accessed=9_000_000, transcendentals=1 << 20),
    )(mask, q, qr, do, s_own, d_own, *slots)


def latent_gradient(which, name, dst, pt, q, qr, do, types):
    rows, width = q.shape
    return pl.pallas_call(
        functools.partial(latent_kernel, 2 * TOK * which, 1024),
        name=name,
        in_specs=[HERE] * 5,
        out_specs=[HERE] * 2,
        out_shape=arrays(*[((TOK, WIDE), t) for t in types]),
        scratch_shapes=[VM((2 * TOK, width), F32), VM((2 * TOK, ROPE), F32)],
        compiler_params=pltpu.CompilerParams(vmem_limit_bytes=24 << 20),
        cost_estimate=pl.CostEstimate(flops=1_200_000_000, bytes_accessed=6_000_000, transcendentals=0),
    )(dst, pt, q, qr, do)


def query_gradient(dst, kcat, kr):
    keys, rows = dst.shape
    width = kcat.shape[1]
    return pl.pallas_call(
        dq_kernel,
        name="query_gradient",
        grid=(rows // ROWS,),
        in_specs=[HERE] * 3,
        out_specs=[
            pl.BlockSpec((ROWS, width), lambda i: (i, 0)), pl.BlockSpec((ROWS, ROPE), lambda i: (i, 0)),
        ],
        out_shape=arrays(((rows, width), BF16), ((rows, ROPE), BF16)),
        compiler_params=pltpu.CompilerParams(vmem_limit_bytes=16 << 20),
        cost_estimate=pl.CostEstimate(flops=2_400_000_000, bytes_accessed=5_000_000, transcendentals=0),
    )(dst, kcat, kr)


def on_device(query_latent_plain, query_rope, latent_nope, latent_rope, latent_output_gradient, block_mask):
    tokens, heads, width = query_latent_plain.shape
    rows = tokens * heads
    sizes = (lax.axis_size("ctx"), lax.axis_size("hg"))
    send = functools.partial(moved, sizes=sizes)
    own = pl.pallas_call(
        pack_kernel,
        name="pack",
        in_specs=[pl.BlockSpec((TOK, width), lambda: (0, 0)), pl.BlockSpec((ROPE, TOK), lambda: (0, 0))],
        out_specs=HERE,
        out_shape=jax.ShapeDtypeStruct((TOK + 16, width), BF16),
        compiler_params=pltpu.CompilerParams(vmem_limit_bytes=4 << 20),
    )(
        pltpu.with_memory_space_constraint(latent_nope, pltpu.HBM),
        pltpu.with_memory_space_constraint(latent_rope.T, pltpu.HBM),
    )
    two = send(own, source=lambda c, h: (c - 2, h))
    mask = lax.dynamic_slice(block_mask, (2 * lax.axis_index("ctx"), 0), (2, block_mask.shape[1]))
    mask, own_far, query_latent_plain, latent_output_gradient = lax.optimization_barrier(
        (mask, own, query_latent_plain, latent_output_gradient)
    )
    far = send(own_far, source=lambda c, h: (far_source(c), h))
    q, do, qr, s_own, d_own = local_scores(
        query_latent_plain.reshape(rows, width),
        latent_output_gradient.reshape(rows, width),
        jnp.transpose(query_rope, (1, 2, 0)),
        own,
    )
    two, q, do, s_own, d_own, qr = lax.optimization_barrier((two, q, do, s_own, d_own, qr))
    swp = send(two, source=lambda c, h: (c ^ 1, h))
    swp, far = lax.optimization_barrier((swp, far))
    dst, pt, kcat, kr = scores(sizes[0], mask, q, qr, do, s_own, d_own, (own, two, far, swp))
    far_dk, swp_dk = latent_gradient(1, "latent_far", dst, pt, q, qr, do, (BF16, BF16))
    got_far = send(far_dk, source=lambda c, h: (far_home(c), h))
    got_swp = send(swp_dk, source=lambda c, h: (c ^ 1, h))
    dst, pt, swp_dk, far_dk = lax.optimization_barrier((dst, pt, swp_dk, far_dk))
    own_dk, two_dk = latent_gradient(0, "latent_near", dst, pt, q, qr, do, (F32, F32))
    two_dk, got_swp = lax.optimization_barrier((two_dk, got_swp))
    two_same = (two_dk[:64] + got_swp[:64].astype(F32)).astype(BF16)
    two_other = (two_dk[64:] + got_swp[64:].astype(F32)).astype(BF16)
    got_two = send(two_same, source=lambda c, h: (c + 2, h))
    got_two_y = send(two_other, source=lambda c, h: (c + 2, h ^ 1))
    own_other = (own_dk[64:] + got_far[64:].astype(F32)).astype(BF16)
    got_own_y = send(own_other, source=lambda c, h: (c, h ^ 1))
    dst, two_same, two_other, own_other = lax.optimization_barrier((dst, two_same, two_other, own_other))
    dq, dqr = query_gradient(dst, kcat, kr)
    dq, dqr, got_two, got_two_y, got_own_y = lax.optimization_barrier((dq, dqr, got_two, got_two_y, got_own_y))
    total = own_dk[:64] + got_far[:64].astype(F32)
    for got in (got_own_y, got_two, got_two_y):
        total = total + got.astype(F32)
    low = total[16:].astype(BF16)
    pieces = [send(low[16 * k - 16 : 16 * k], source=lambda c, h, k=k: (c, (h - 2 * k) % 8)) for k in (2, 3, 1)]
    nope, rope = pl.pallas_call(
        finish_kernel,
        name="finish",
        out_shape=[jax.ShapeDtypeStruct((16, width), F32), jax.ShapeDtypeStruct((16, ROPE), F32)],
        compiler_params=pltpu.CompilerParams(vmem_limit_bytes=2 << 20),
    )(total[:16], *pieces)
    return (dq.reshape(tokens, heads, width), dqr.reshape(tokens, heads, ROPE), nope, rope)


def solution(mesh):
    in_specs = (
        P("ctx", "hg", None), P("ctx", "hg", None), P("ctx", None), P("ctx", None), P("ctx", "hg", None), P(),
    )
    out_specs = (P("ctx", "hg", None), P("ctx", "hg", None), P(("ctx", "hg"), None), P(("ctx", "hg"), None))
    return jax.shard_map(on_device, mesh=mesh, in_specs=in_specs, out_specs=out_specs, check_vma=False)
```
